512 devices in a mesh: row: 16 (over z_hi, y, core), col: 32 (over z_lo, x).
Axes of the slice: x: 4, y: 4, z: 16 (z_hi: 2, z_lo: 8; z = z_hi * 8 + z_lo), core: 2. Of those that a mesh axis runs over, the one named last changes fastest.
Arguments:
- object_field: float32 [2, 2048, 4096], P(None, 'row', 'col'), may hold values from -6 to 6
- probe_mode_stack: float32 [2, 4, 128, 128], replicated, may hold values from -6 to 6
- measured: float32 [16, 32, 4, 128, 128], P('row', 'col'), may hold values from 1 to 7
- positions: int32 [16, 32, 4, 2], P('row', 'col'), may hold values from 0 to 128
- counts: int32 [16, 32], P('row', 'col'), may hold values from 1 to 4, as said below
Outputs:
- new_object: float32 [2, 2048, 4096], P(None, 'row', 'col')
- probe_step: float32 [2, 4, 128, 128], replicated
The draws below stay inside these ranges and needn't reach their ends.
Inputs may be any that keep to these rules, and one draw needn't show every extreme that they name: `positions`: each frame lies inside its tile extended by 64 cells on each side. A tile's live frames are its first counts slots; some tile uses all 4 slots.
All inputs are finite; a program needn't handle non-finite values.
Results may differ from the reference program's by a relative error of at most 0.0003.
Values sent between devices are 32-bit elements; how exact they have to be, the bound alone decides.
No kernel may reach another device: no remote copies, remote signals or barrier semaphores. Data moves between devices by JAX's collectives and lax.ppermute only.
A program may use at most 64 MiB of HBM per device.

```python
import jax
import jax.numpy as jnp
from jax import lax

FRAME_PIXELS = 128
MODES = 4
HALO = 64
TILE = 128
SLOTS = 4
TILE_ROWS = 16
TILE_COLS = 32
NY = 2048
NX = 4096


def draw_counts(key, part):
    first_key, second_key = jax.random.split(jax.random.fold_in(key, 11))
    tiles_all = TILE_ROWS * TILE_COLS
    base_counts = jax.random.randint(first_key, (tiles_all,), 1, SLOTS + 1)
    full_spot = jax.random.randint(second_key, (), 0, tiles_all)
    base_counts = jnp.where(jnp.arange(tiles_all) == full_spot, SLOTS, base_counts)
    return base_counts.reshape(TILE_ROWS, TILE_COLS).astype(jnp.int32)


def plant(entries, rng, low, high):
    longest = entries.shape.index(max(entries.shape))
    spots = []
    for shift in (0, 1):
        where = [jax.random.randint(jax.random.fold_in(rng, axis), (), 0, length) for axis, length in enumerate(entries.shape)]
        where[longest] = (where[longest] + shift) % entries.shape[longest]
        spots.append(tuple(where))
    return entries.at[spots[0]].set(low).at[spots[1]].set(high)


def shard_levels(key, shape, cuts, smallest, high):
    factor_of, own = 1.0, jax.random.fold_in(key, 6)
    for position, shards_of in cuts:
        steps = jnp.exp(jax.random.uniform(jax.random.fold_in(own, position), (shards_of,), jnp.float32, smallest / len(cuts), high / len(cuts)))
        factor_of = factor_of * jnp.repeat(steps, shape[position] // shards_of).reshape([-1 if axis == position else 1 for axis in range(len(shape))])
    return factor_of


def normal_values(stream_key, shape, spread, reach, cuts=(), kind=jnp.bfloat16):
    drawn = jax.random.normal(stream_key, shape, jnp.float32) * spread
    if len(cuts) > 0:
        drawn = shard_levels(stream_key, shape, cuts, -0.22, 0.18) * drawn
    return jnp.clip(drawn, min=-reach, max=reach).astype(kind)


def setup_inputs(seed: int = 0) -> dict:
    arg_keys = jax.random.split(jax.random.key(seed), 6)
    object_field = normal_values(arg_keys[0], (2, NY, NX), 1.0, 6.0, ((1, 16), (2, 32)), jnp.float32)
    probe_mode_stack = normal_values(arg_keys[1], (2, MODES, FRAME_PIXELS, FRAME_PIXELS), 1.0, 6.0, (), jnp.float32)
    measured = jnp.clip(1.0 + 6.0 * jax.random.uniform(arg_keys[2], (TILE_ROWS, TILE_COLS, SLOTS, FRAME_PIXELS, FRAME_PIXELS), jnp.float32) ** shard_levels(arg_keys[2], (TILE_ROWS, TILE_COLS, SLOTS, FRAME_PIXELS, FRAME_PIXELS), ((0, 16), (1, 32)), -0.2, 0.2), 1.0, 7.0)
    positions = plant(jax.random.randint(arg_keys[3], (TILE_ROWS, TILE_COLS, SLOTS, 2), 0, TILE + 2 * HALO - FRAME_PIXELS + 1), jax.random.fold_in(arg_keys[3], 1), 0, TILE + 2 * HALO - FRAME_PIXELS).astype(jnp.int32)
    counts = draw_counts(jax.random.fold_in(arg_keys[5], 71), 0)
    return dict(object_field=object_field, probe_mode_stack=probe_mode_stack, measured=measured, positions=positions, counts=counts)


def reference(object_field, probe_mode_stack, measured, positions, counts):
    padded = jnp.pad(object_field, ((0, 0), (HALO, HALO), (HALO, HALO)))
    probe_wave = probe_mode_stack[0] + 1j * probe_mode_stack[1]
    illumination = lax.optimization_barrier(jnp.sum(probe_mode_stack * probe_mode_stack, axis=(0, 1)))
    per_tile_row = TILE_COLS * SLOTS
    slot_total_count = TILE_ROWS * per_tile_row
    flat_pos = positions.reshape(slot_total_count, 2).astype(jnp.int32)
    flat_measured = measured.reshape(slot_total_count, FRAME_PIXELS, FRAME_PIXELS)
    slot_ids = jnp.arange(slot_total_count, dtype=jnp.int32)
    tile_row = (slot_ids // per_tile_row).astype(jnp.int32)
    tile_col = (slot_ids // SLOTS % TILE_COLS).astype(jnp.int32)
    slot_number = (slot_ids % SLOTS).astype(jnp.int32)
    active_mask = (slot_number < counts[tile_row, tile_col]).astype(object_field.dtype)
    row_begin = (tile_row * TILE + flat_pos[:, 0]).astype(jnp.int32)
    column_begin = (tile_col * TILE + flat_pos[:, 1]).astype(jnp.int32)
    zero_index = jnp.zeros((), jnp.int32)

    def visit_frame(carry, input_arrays):
        grad_pad, probe_sum, cover_sum = carry
        row_first, column_first, measured_amplitude, active_value = input_arrays
        row_first = row_first.astype(jnp.int32)
        column_first = column_first.astype(jnp.int32)
        object_window = lax.dynamic_slice(padded, (zero_index, row_first, column_first), (2, FRAME_PIXELS, FRAME_PIXELS))
        patch_wave = object_window[0] + 1j * object_window[1]
        exit_wave = probe_wave * patch_wave
        far_field = jnp.fft.fft2(exit_wave, norm='ortho')
        far_re = jnp.real(far_field)
        far_im = jnp.imag(far_field)
        model_intensity = lax.optimization_barrier(jnp.sum(far_re * far_re + far_im * far_im, axis=0))
        frame_weight = 1.0 - measured_amplitude / jnp.sqrt(model_intensity + 1.0)
        back_wave = jnp.fft.ifft2(far_field * frame_weight, norm='ortho')
        object_grad = lax.optimization_barrier(jnp.sum(jnp.conj(probe_wave) * back_wave, axis=0))
        local_terms = jnp.stack([jnp.real(object_grad), jnp.imag(object_grad), illumination]) * active_value
        current = lax.dynamic_slice(grad_pad, (zero_index, row_first, column_first), (3, FRAME_PIXELS, FRAME_PIXELS))
        grad_pad = lax.dynamic_update_slice(grad_pad, current + local_terms, (zero_index, row_first, column_first))
        probe_grad = jnp.conj(patch_wave) * back_wave
        probe_sum = probe_sum + jnp.stack([jnp.real(probe_grad), jnp.imag(probe_grad)]) * active_value
        cover_sum = cover_sum + (object_window[0] * object_window[0] + object_window[1] * object_window[1]) * active_value
        return ((grad_pad, probe_sum, cover_sum), None)
    initial_state = (jnp.zeros((3, NY + 2 * HALO, NX + 2 * HALO), object_field.dtype), jnp.zeros(probe_mode_stack.shape, object_field.dtype), jnp.zeros((FRAME_PIXELS, FRAME_PIXELS), object_field.dtype))
    running_totals, unused_value = lax.scan(visit_frame, initial_state, (row_begin, column_begin, flat_measured, active_mask))
    grad_pad, probe_sum, cover_sum = running_totals
    interior = grad_pad[:, HALO:HALO + NY, HALO:HALO + NX]
    new_object = object_field - interior[:2] / (interior[2:3] + 1.0)
    probe_step = probe_sum / jnp.sqrt(cover_sum + 1.0)
    return (new_object, probe_step)
```

```python
import functools
import math

import jax
import jax.numpy as jnp
import ml_dtypes
import numpy as np
from jax import lax
from jax.experimental import pallas as pl
from jax.experimental.pallas import tpu as pltpu
from jax.sharding import Mesh, PartitionSpec as P

HALO = 64
SIDE = 128
MODES = 4
SLOTS = 4
EXT = 256

ROW = ("zh", "y", "c")
COL = ("zl", "x")
PLANE = ("c", "y", "x")
DEPTH = ("zh", "zl")


def pairs(count):
    even = [(i, i ^ 1) for i in range(count)]
    odd = [(i, i + 1) for i in range(1, count - 1, 2)]
    return even, odd + [(b, a) for a, b in odd]


def dft_tables():
    k = np.arange(SIDE)
    angle = (k[:, None] * k[None, :] % SIDE) * (2.0 * math.pi / SIDE)
    c = np.cos(angle) / math.sqrt(SIDE)
    s = np.sin(angle) / math.sqrt(SIDE)
    r = np.block([[c, -s], [s, c]])
    l = np.block([[c, s], [-s, c]])

    def split(m):
        hi = m.astype(np.float32).astype(ml_dtypes.bfloat16)
        lo = (m - hi.astype(np.float64)).astype(np.float32).astype(ml_dtypes.bfloat16)
        return hi, lo

    (rh, rl), (lh, ll) = split(r), split(l)
    return np.stack([rh, rl, lh, ll])


def low_lanes(rows):
    return lax.broadcasted_iota(jnp.int32, (rows, SIDE), 1) < HALO


def half(v):
    return pltpu.roll(v, HALO, axis=1)


def hi_lo(x):
    hi = x.astype(jnp.bfloat16)
    lo = (x - hi.astype(jnp.float32)).astype(jnp.bfloat16)
    return hi, lo


def pack_kernel(par, own, row_e, row_o, vext, send_e, send_o):
    c, x = par[0], par[1]
    for q in range(2):
        vext[q, HALO : HALO + SIDE, :] = own[q]

    @pl.when(c == 0)
    def _():
        vext[:, 0:HALO, :] = row_o[...]
        vext[:, HALO + SIDE :, :] = row_e[...]

    @pl.when(c == 1)
    def _():
        vext[:, 0:HALO, :] = row_e[...]
        vext[:, HALO + SIDE :, :] = row_o[...]

    lo = low_lanes(EXT)
    re, im = vext[0], vext[1]
    left = jnp.where(lo, re, half(im))
    right = jnp.where(lo, half(re), im)
    even = x == 0
    send_e[...] = jnp.where(even, right, left)
    send_o[...] = jnp.where(even, left, right)


def frames_kernel(
    scal, vext, col_e, col_o, probe, measured, tables, payload, send_e, send_o, mid, ext, gext, illum
):
    x = scal[9]
    count = scal[8]
    lo = low_lanes(EXT)
    even = x == 0
    left = jnp.where(even, col_o[...], col_e[...])
    right = jnp.where(even, col_e[...], col_o[...])
    re, im = half(vext[0]), half(vext[1])
    ext[0, :EXT, :SIDE] = jnp.where(lo, left, re)
    ext[0, :EXT, SIDE:] = jnp.where(lo, re, half(right))
    ext[1, :EXT, :SIDE] = jnp.where(lo, half(left), im)
    ext[1, :EXT, SIDE:] = jnp.where(lo, im, right)
    ext[:, EXT:, :] = jnp.zeros((2, 8, EXT), jnp.float32)
    gext[...] = jnp.zeros(gext.shape, jnp.float32)
    payload[...] = jnp.zeros(payload.shape, jnp.float32)
    total = probe[0, 0] * probe[0, 0] + probe[1, 0] * probe[1, 0]
    for m in range(1, MODES):
        total = total + probe[0, m] * probe[0, m] + probe[1, m] * probe[1, m]
    illum[...] = total
    rh, rl, lh, ll = tables[0], tables[1], tables[2], tables[3]

    def times_right(v, wh, wl):
        hi, low = hi_lo(v)
        lhs = jnp.concatenate([hi, low, hi], axis=1)
        rhs = jnp.concatenate([wh, wh, wl], axis=0)
        return jnp.dot(lhs, rhs, preferred_element_type=jnp.float32)

    def times_left(wh, wl, v):
        hi, low = hi_lo(v)
        lhs = jnp.concatenate([wh, wh, wl], axis=1)
        rhs = jnp.concatenate([hi, low, hi], axis=0)
        return jnp.dot(lhs, rhs, preferred_element_type=jnp.float32)

    def to_columns(v):
        return jnp.concatenate(
            [
                jnp.concatenate(
                    [v[m * SIDE : (m + 1) * SIDE, :SIDE], v[m * SIDE : (m + 1) * SIDE, SIDE:]], axis=0
                )
                for m in range(MODES)
            ],
            axis=1,
        )

    def to_rows(v):
        return jnp.concatenate(
            [
                jnp.concatenate(
                    [v[:SIDE, m * SIDE : (m + 1) * SIDE], v[SIDE:, m * SIDE : (m + 1) * SIDE]], axis=1
                )
                for m in range(MODES)
            ],
            axis=0,
        )

    def frame(s, carry):
        row, col = scal[2 * s], scal[2 * s + 1]
        offset = lax.rem(row, 8)
        rows = pl.ds(pl.multiple_of(row - offset, 8), SIDE + 8)
        col_back = lax.rem(EXT - col, EXT)
        row_back = lax.rem(SIDE + 8 - offset, SIDE + 8)

        def cut(q):
            wide = pltpu.roll(ext[q, rows, :], col_back, axis=1)[:, :SIDE]
            return pltpu.roll(wide, row_back, axis=0)[:SIDE]

        patch_re, patch_im = cut(0), cut(1)
        waves = []
        for m in range(MODES):
            pr, pi = probe[0, m], probe[1, m]
            waves.append(
                jnp.concatenate([pr * patch_re - pi * patch_im, pr * patch_im + pi * patch_re], axis=1)
            )
        wave = jnp.concatenate(waves, axis=0)
        far = times_left(lh, ll, to_columns(times_right(wave, rh, rl)))
        power = far * far
        power = power[:SIDE] + power[SIDE:]
        intensity = power[:, :SIDE]
        for m in range(1, MODES):
            intensity = intensity + power[:, m * SIDE : (m + 1) * SIDE]
        weight = 1.0 - measured[s] / jnp.sqrt(intensity + 1.0)
        weight = jnp.concatenate([weight] * MODES, axis=1)
        far = far * jnp.concatenate([weight, weight], axis=0)
        back = times_right(to_rows(times_left(rh, rl, far)), lh, ll)
        grad_re = jnp.zeros((SIDE, SIDE), jnp.float32)
        grad_im = jnp.zeros((SIDE, SIDE), jnp.float32)
        for m in range(MODES):
            pr, pi = probe[0, m], probe[1, m]
            br = back[m * SIDE : (m + 1) * SIDE, :SIDE]
            bi = back[m * SIDE : (m + 1) * SIDE, SIDE:]
            grad_re = grad_re + (pr * br + pi * bi)
            grad_im = grad_im + (pr * bi - pi * br)
            payload[0, :, m] += (patch_re * br + patch_im * bi).reshape(16, 8, SIDE)
            payload[1, :, m] += (patch_re * bi - patch_im * br).reshape(16, 8, SIDE)
        payload[0, :, MODES] += (patch_re * patch_re + patch_im * patch_im).reshape(16, 8, SIDE)
        margin = jnp.zeros((8, SIDE), jnp.float32)
        blank = jnp.zeros((SIDE + 8, SIDE), jnp.float32)
        for q, part in enumerate((grad_re, grad_im, illum[...])):
            tall = pltpu.roll(jnp.concatenate([part, margin], axis=0), offset, axis=0)
            gext[q, rows, :] += pltpu.roll(jnp.concatenate([tall, blank], axis=1), col, axis=1)
        return carry

    lax.fori_loop(0, count, frame, 0)
    payload[1, :, MODES] = payload[0, :, MODES]

    lo_half = low_lanes(SIDE)
    first = [gext[q, :EXT, :SIDE] for q in range(3)]
    second = [gext[q, :EXT, SIDE:] for q in range(3)]
    left = jnp.where(lo, first[0], half(first[1]))
    left_i = jnp.where(lo_half, first[2][:SIDE], half(first[2][SIDE:]))
    right = jnp.where(lo, half(second[0]), second[1])
    right_i = jnp.where(lo_half, half(second[2][:SIDE]), second[2][SIDE:])
    send_e[:EXT] = jnp.where(even, right, left)
    send_e[EXT:] = jnp.where(even, right_i, left_i)
    send_o[:EXT] = jnp.where(even, left, right)
    send_o[EXT:] = jnp.where(even, left_i, right_i)
    for q in range(3):
        mid[q] = jnp.where(lo, half(first[q]), half(second[q]))


def columns_kernel(par, mid, col_e, col_o, send_e, send_o, inner):
    c, x = par[0], par[1]
    even = x == 0
    lo = low_lanes(EXT)
    lo_half = low_lanes(SIDE)
    from_right = jnp.where(even, col_e[...], col_o[...])
    from_left = jnp.where(even, col_o[...], col_e[...])
    swap_right, swap_left = half(from_right), half(from_left)
    add_re = jnp.where(lo, from_left[:EXT], swap_right[:EXT])
    add_im = jnp.where(lo, swap_left[:EXT], from_right[:EXT])
    add_top = jnp.where(lo_half, from_left[EXT:], swap_right[EXT:])
    add_bottom = jnp.where(lo_half, swap_left[EXT:], from_right[EXT:])
    add_illum = jnp.concatenate([add_top, add_bottom], axis=0)
    even_row = c == 0
    for q, add in enumerate((add_re, add_im, add_illum)):
        total = mid[q] + add
        top, bottom = total[:HALO], total[EXT - HALO :]
        inner[q] = total[HALO : HALO + SIDE]
        send_e[q] = jnp.where(even_row, bottom, top)
        send_o[q] = jnp.where(even_row, top, bottom)


def object_kernel(par, inner, row_e, row_o, own, new):
    even = par[0] == 0
    below = jnp.where(even, row_e[...], row_o[...])
    above = jnp.where(even, row_o[...], row_e[...])
    for part, extra in ((0, above), (1, below)):
        rows = pl.ds(part * HALO, HALO)
        total = [inner[q, rows, :] + extra[q] for q in range(3)]
        step = total[2] + 1.0
        for q in range(2):
            new[q, rows, :] = own[q, rows, :] - total[q] / step


def f32(*shape):
    return jax.ShapeDtypeStruct(shape, jnp.float32)


SMEM = pl.BlockSpec(memory_space=pltpu.SMEM)
VMEM = pl.BlockSpec(memory_space=pltpu.VMEM)


def per_device(own, probe, measured, positions, counts):
    row_even, row_odd = pairs(16)
    col_even, col_odd = pairs(32)
    c = lax.axis_index("c").astype(jnp.int32)
    x = (lax.axis_index("x") % 2).astype(jnp.int32)
    par = jnp.stack([c, x])
    scal = jnp.concatenate([positions.reshape(2 * SLOTS), counts.reshape(1), x.reshape(1)])
    top, bottom = own[:, :HALO], own[:, HALO:]
    row_o = lax.ppermute(jnp.where(c == 0, top, bottom), ROW, row_odd)
    row_e = lax.ppermute(jnp.where(c == 0, bottom, top), ROW, row_even)
    vext, send_e, send_o = pl.pallas_call(
        pack_kernel,
        out_shape=(f32(2, EXT, SIDE), f32(EXT, SIDE), f32(EXT, SIDE)),
        in_specs=[SMEM, VMEM, VMEM, VMEM],
        out_specs=(VMEM, VMEM, VMEM),
        name="pack",
    )(par, own, row_e, row_o)
    col_o = lax.ppermute(send_o, COL, col_odd)
    col_e = lax.ppermute(send_e, COL, col_even)
    payload, send_e, send_o, mid = pl.pallas_call(
        frames_kernel,
        out_shape=(f32(2, 16, 5, 8, SIDE), f32(384, SIDE), f32(384, SIDE), f32(3, EXT, SIDE)),
        in_specs=[SMEM] + [VMEM] * 6,
        out_specs=(VMEM,) * 4,
        scratch_shapes=[
            pltpu.VMEM((2, EXT + 8, EXT), jnp.float32),
            pltpu.VMEM((3, EXT + 8, EXT), jnp.float32),
            pltpu.VMEM((SIDE, SIDE), jnp.float32),
        ],
        name="frames",
    )(scal, vext, col_e, col_o, probe, measured[0, 0], jnp.asarray(dft_tables()))

    col_o = lax.ppermute(send_o, COL, col_odd)
    col_e = lax.ppermute(send_e, COL, col_even)
    spread = lax.all_to_all(payload.reshape(32, 40, SIDE), PLANE, 0, 0, tiled=True)
    chunk = jnp.sum(spread, axis=0)
    send_e, send_o, inner = pl.pallas_call(
        columns_kernel,
        out_shape=(f32(3, HALO, SIDE), f32(3, HALO, SIDE), f32(3, SIDE, SIDE)),
        in_specs=[SMEM, VMEM, VMEM, VMEM],
        out_specs=(VMEM, VMEM, VMEM),
        name="columns",
    )(par, mid, col_e, col_o)
    row_o = lax.ppermute(send_o, ROW, row_odd)
    row_e = lax.ppermute(send_e, ROW, row_even)
    spread = lax.all_to_all(jnp.broadcast_to(chunk, (16, 40, SIDE)), DEPTH, 0, 0, tiled=True)
    chunk = jnp.sum(spread, axis=0)
    sums, cover = chunk[:32].reshape(MODES, 8, SIDE), chunk[32:]
    step = (sums / jnp.sqrt(cover + 1.0)).reshape(32, SIDE)
    gathered = lax.all_to_all(jnp.broadcast_to(step, (32, 32, SIDE)), PLANE, 0, 0, tiled=True)
    probe_step = gathered.reshape(2, 16, MODES, 8, SIDE).transpose(0, 2, 1, 3, 4)
    new_object = pl.pallas_call(
        object_kernel,
        out_shape=f32(2, SIDE, SIDE),
        in_specs=[SMEM] + [VMEM] * 4,
        out_specs=VMEM,
        name="object",
    )(par, inner, row_e, row_o, own)
    return new_object, probe_step.reshape(2, MODES, SIDE, SIDE)


def solution(mesh):
    fine = Mesh(mesh.devices.reshape(2, 4, 2, 8, 4), ("zh", "y", "c", "zl", "x"))
    return jax.shard_map(
        per_device,
        mesh=fine,
        in_specs=(
            P(None, ROW, COL),
            P(),
            P(ROW, COL, None, None, None),
            P(ROW, COL, None, None),
            P(ROW, COL),
        ),
        out_specs=(P(None, ROW, COL), P()),
        check_vma=False,
    )
```
